32 devices in a mesh: expert: 8 (over z, y), ctx: 4 (over x, core).
Axes of the slice: x: 2, y: 2, z: 4, core: 2. Of those that a mesh axis runs over, the one named last changes fastest.
Arguments:
- resid: bfloat16 [4096, 2048], P(('expert', 'ctx')), may hold values from -30 to 30
- queries: bfloat16 [4096, 2048], P(('expert', 'ctx')), may hold values from -8 to 8
- keys: bfloat16 [4096, 2048], P(('expert', 'ctx')), may hold values from -8 to 8
- values: bfloat16 [4096, 2048], P(('expert', 'ctx')), may hold values from -6 to 6
- mod_scale: float32 [8, 2048], P('expert'), may hold values from -0.5 to 0.5
- mod_shift: float32 [8, 2048], P('expert'), may hold values from -3 to 3
- mod_gate: float32 [8, 2048], P('expert'), may hold values from 0.5 to 1.5
- router: bfloat16 [2048, 8], replicated, may hold values from -0.125 to 0.125
- w_in: bfloat16 [8, 2048, 1024], P('expert', None, 'ctx'), may hold values from -0.125 to 0.125
- w_out: bfloat16 [8, 1024, 2048], P('expert', 'ctx'), may hold values from -0.1875 to 0.1875
- expert_ids: int32 [4096, 2], P(('expert', 'ctx')), may hold values from 0 to 7, all different within a row; in each aligned block of 128 rows (0 to 127, 128 to 255, ...) at most 40 rows name the same one
- grad_out: bfloat16 [4096, 2048], P(('expert', 'ctx')), may hold values from -1.5 to 1.5
Outputs:
- mixed_out: bfloat16 [4096, 2048], P(('expert', 'ctx'))
- resid_grad: bfloat16 [4096, 2048], P(('expert', 'ctx'))
- grad_queries: bfloat16 [4096, 2048], P(('expert', 'ctx'))
- grad_keys: bfloat16 [4096, 2048], P(('expert', 'ctx'))
- grad_values: bfloat16 [4096, 2048], P(('expert', 'ctx'))
- grad_w_in: bfloat16 [8, 2048, 1024], P('expert', None, 'ctx')
- grad_w_out: bfloat16 [8, 1024, 2048], P('expert', 'ctx')
- grad_router: float32 [2048, 8], replicated
The draws below stay inside these ranges and needn't reach their ends.
Inputs may be any that keep to these rules, and one draw needn't show every extreme that they name: `expert_ids`: each token names two different experts. Within one aligned block of 128 tokens no expert is named by more than 40 tokens, and some block reaches 40.
All inputs are finite; a program needn't handle non-finite values.
Results may differ from the reference program's by a relative error of at most 0.013.
The reference program's roundings to bfloat16 on the way count: a program that leaves them out, or rounds other values in their place, can miss the bound.
Values may be sent and summed in bfloat16 or wider, within the bound.
A program may use at most 128 MiB of HBM per device.

```python
import math
import jax
import jax.numpy as jnp
import numpy as np
from jax import lax

D = 2048
HEADS = 16
HDIM = 128
FF = 1024
EXPERTS = 8
TOK_DEV = 128
CLIP = 512
CLIPS = 8
TOKENS = 4096
CAP = 40
FF_BLOCK = 256
N_CTX = 4


def draw_resid(key, part):
    row_key, col_key, base_key = jax.random.split(key, 3)
    row_scale = jnp.exp(jax.random.uniform(row_key, (TOKENS, 1), minval=math.log(0.25), maxval=math.log(2.5)))
    col_scale = jnp.exp(jax.random.uniform(col_key, (1, D), minval=math.log(0.3), maxval=math.log(3.0)))
    base_values = jax.random.normal(base_key, (TOKENS, D))
    return jnp.clip(base_values * row_scale * col_scale, -30.0, 30.0).astype(jnp.bfloat16)


def paired_heads(key):
    folded = jax.random.fold_in(key, 11)
    split_keys = jax.random.split(folded, 2)
    query_values = jnp.clip(jax.random.normal(split_keys[0], (TOKENS, D)), -8.0, 8.0)
    key_values = jnp.clip(jax.random.normal(split_keys[1], (TOKENS, D)), -8.0, 8.0)
    return (query_values.astype(jnp.bfloat16), key_values.astype(jnp.bfloat16))


def draw_queries(key, part):
    return paired_heads(key)[0]


def draw_keys(key, part):
    return paired_heads(key)[1]


def shard_levels(stream_key, extent, cuts, low, top_value):
    factor_of = 1.0
    for dim, shards_of in cuts:
        draws = jax.random.uniform(jax.random.fold_in(jax.random.fold_in(stream_key, 6), dim), (shards_of,), jnp.float32, low / len(cuts), top_value / len(cuts))
        factor_of = factor_of * jnp.repeat(jnp.exp(draws), extent[dim] // shards_of).reshape((-1,) + (1,) * (len(extent) - 1 - dim))
    return factor_of


def routed_block(stream_key, own, number, rows, amount, top, bound, skew):
    order = jax.random.permutation(stream_key, amount)
    heavy_load, ordinary = shares(amount, rows * top, bound, skew, True), shares(amount, rows * top, bound, skew, False)
    places = jnp.arange(amount)

    def named(tallies, turn):
        used = int((tallies > 0).sum())
        fixed = max(1, used // 4)
        shifted = fixed + (places - fixed + turn * (used - fixed)) % max(1, amount - fixed)
        return jnp.zeros((amount,), jnp.int32).at[order[jnp.where(places < fixed, places, shifted)]].set(jnp.asarray(tallies, jnp.int32))

    tallies = jnp.where(number % 4 == 0, named(heavy_load, number // 4), named(ordinary, number - number // 4 - 1))
    mixed = jax.random.permutation(jax.random.fold_in(own, 3), amount)
    giver, taker = mixed[0:amount // 2 * 2:2], mixed[1:amount // 2 * 2:2]
    room = jnp.minimum(tallies[giver] - 1, bound - tallies[taker]) // 2
    room = jnp.where((giver == order[0]) | (taker == order[0]) | (tallies[taker] == 0), 0, jnp.maximum(room, 0))
    shifted = jax.random.randint(jax.random.fold_in(own, 4), (amount // 2,), 0, 1 << 20) % (room + 1)
    tallies = tallies.at[giver].add(-shifted).at[taker].add(shifted)
    members = jnp.searchsorted(jnp.cumsum(tallies), jnp.arange(rows * top), side="right").astype(jnp.int32)
    table = members.reshape(top, rows).T
    table = table[jax.random.permutation(jax.random.fold_in(own, 1), rows)]
    turn = jax.random.randint(jax.random.fold_in(own, 2), (rows, 1), 0, top)
    return jnp.take_along_axis(table, (jnp.arange(top)[None, :] + turn) % top, axis=1)


def shares(number_of, total, reach, skew, full):
    portions = [(1 << 20) // math.isqrt(grade ** skew) + 1 for grade in range(1, number_of + 1)]
    largest = reach if full else min(reach, max(-(-total // number_of), total * portions[0] // sum(portions)))
    least = 1 if total - largest >= number_of - 1 else 0
    counts, spare = [largest] + [least] * (number_of - 1), total - largest - least * (number_of - 1)
    while spare > 0:
        candidates = [i for i in range(1, number_of) if counts[i] < largest] or [i for i in range(1, number_of) if counts[i] < reach]
        whole, remaining = sum([portions[i] for i in candidates]), spare
        for i in candidates:
            extra = min(reach - counts[i], max(1, remaining * portions[i] // whole), spare)
            counts[i] = counts[i] + extra
            spare = spare - extra
    return np.array(counts)


def centred(stream_key, dims, spread, reach, cuts=(), kind=jnp.bfloat16):
    factor_of = shard_levels(stream_key, dims, cuts, -0.22, 0.18) if cuts else 1.0
    drawn = jax.random.normal(stream_key, dims, jnp.float32) * spread * factor_of
    return jnp.minimum(jnp.maximum(drawn, -reach), reach).astype(kind)


def setup_inputs(seed: int = 0) -> dict:
    arg_keys = jax.random.split(jax.random.key(seed), 13)
    resid = draw_resid(jax.random.fold_in(arg_keys[12], 71), 0)
    queries = draw_queries(jax.random.fold_in(arg_keys[12], 71), 0)
    keys = draw_keys(jax.random.fold_in(arg_keys[12], 71), 0)
    values = centred(arg_keys[3], (TOKENS, D), 1.0, 6.0, ((0, 32),))
    mod_scale = jnp.clip(jax.random.uniform(arg_keys[4], (CLIPS, D), jnp.float32, -0.5, 0.5) * shard_levels(arg_keys[4], (CLIPS, D), ((0, 8),), -0.4, 0.0), -0.5, 0.5)
    mod_shift = centred(arg_keys[5], (CLIPS, D), 0.5, 3.0, ((0, 8),), jnp.float32)
    mod_gate = jnp.clip(0.5 + 1.0 * jax.random.uniform(arg_keys[6], (CLIPS, D), jnp.float32) ** shard_levels(arg_keys[6], (CLIPS, D), ((0, 8),), -0.2, 0.2), 0.5, 1.5)
    router = centred(arg_keys[7], (D, EXPERTS), D ** -0.5, 0.125)
    w_in = centred(arg_keys[8], (EXPERTS, D, FF), D ** -0.5, 0.125, ((0, 8), (2, 4)))
    w_out = centred(arg_keys[9], (EXPERTS, FF, D), FF ** -0.5, 0.1875, ((0, 8), (1, 4)))
    expert_ids_keys = jax.random.split(jax.random.fold_in(arg_keys[10], 1), TOKENS // TOK_DEV)
    expert_ids_turns = jax.random.permutation(jax.random.fold_in(arg_keys[10], 3), TOKENS // TOK_DEV)
    expert_ids = jax.vmap(lambda own, number: routed_block(jax.random.fold_in(arg_keys[10], 2), own, number, TOK_DEV, EXPERTS, 2, CAP, 2))(expert_ids_keys, expert_ids_turns).reshape((TOKENS, 2))
    grad_out = centred(arg_keys[11], (TOKENS, D), 0.25, 1.5, ((0, 32),))
    return dict(resid=resid, queries=queries, keys=keys, values=values, mod_scale=mod_scale, mod_shift=mod_shift, mod_gate=mod_gate, router=router, w_in=w_in, w_out=w_out, expert_ids=expert_ids, grad_out=grad_out)


NORM_EPSILON = 1e-06

def rounded(value):
    return lax.optimization_barrier(value.astype(jnp.bfloat16)).astype(jnp.float32)

def attend_clip(clip_item):
    query_clip, key_clip, value_clip = clip_item
    score_scale = 1.0 / math.sqrt(HDIM)
    query_heads = query_clip.astype(jnp.float32).reshape(CLIP, HEADS, HDIM)
    key_heads = key_clip.astype(jnp.float32).reshape(CLIP, HEADS, HDIM)
    value_heads = value_clip.astype(jnp.float32).reshape(CLIP, HEADS, HDIM)
    scores = jnp.einsum('qhd,khd->hqk', query_heads, key_heads) * score_scale
    row_top = lax.optimization_barrier(jnp.max(scores, axis=-1))
    exp_scores = jnp.exp(scores - row_top[..., None])
    row_total = lax.optimization_barrier(jnp.sum(exp_scores, axis=-1))
    mixed_values = jnp.einsum('hqk,khd->qhd', rounded(exp_scores), value_heads)
    attn = (mixed_values / row_total.T[:, :, None]).astype(jnp.bfloat16).reshape(CLIP, D)
    return (attn, row_top + jnp.log(row_total))

def attend_back(clip_item):
    query_clip, key_clip, value_clip, attn_clip, log_clip, grad_clip = clip_item
    score_scale = 1.0 / math.sqrt(HDIM)
    query_heads = query_clip.astype(jnp.float32).reshape(CLIP, HEADS, HDIM)
    key_heads = key_clip.astype(jnp.float32).reshape(CLIP, HEADS, HDIM)
    value_heads = value_clip.astype(jnp.float32).reshape(CLIP, HEADS, HDIM)
    attn_heads = attn_clip.astype(jnp.float32).reshape(CLIP, HEADS, HDIM)
    grad_heads = grad_clip.astype(jnp.float32).reshape(CLIP, HEADS, HDIM)
    scores = jnp.einsum('qhd,khd->hqk', query_heads, key_heads) * score_scale
    prob = jnp.exp(scores - log_clip[..., None])
    value_pull = jnp.einsum('qhd,khd->hqk', grad_heads, value_heads)
    row_dot = jnp.einsum('qhd,qhd->hq', grad_heads, attn_heads)
    score_grad = rounded(prob * (value_pull - row_dot[..., None]))
    grad_query = (jnp.einsum('hqk,khd->qhd', score_grad, key_heads) * score_scale).astype(jnp.bfloat16).reshape(CLIP, D)
    grad_blocks = score_grad.reshape(HEADS, N_CTX, TOK_DEV, CLIP)
    prob_blocks = rounded(prob).reshape(HEADS, N_CTX, TOK_DEV, CLIP)
    query_blocks = query_heads.reshape(N_CTX, TOK_DEV, HEADS, HDIM)
    grad_head_blocks = grad_heads.reshape(N_CTX, TOK_DEV, HEADS, HDIM)
    key_parts = rounded(jnp.einsum('hbqk,bqhd->bkhd', grad_blocks, query_blocks) * score_scale)
    value_parts = rounded(jnp.einsum('hbqk,bqhd->bkhd', prob_blocks, grad_head_blocks))
    grad_key = lax.optimization_barrier(jnp.sum(key_parts, axis=0)).astype(jnp.bfloat16).reshape(CLIP, D)
    grad_value = lax.optimization_barrier(jnp.sum(value_parts, axis=0)).astype(jnp.bfloat16).reshape(CLIP, D)
    return (grad_query, grad_key, grad_value)

def reference(resid, queries, keys, values, mod_scale, mod_shift, mod_gate, router, w_in, w_out, expert_ids, grad_out):
    query_clips = queries.reshape(CLIPS, CLIP, D)
    key_clips = keys.reshape(CLIPS, CLIP, D)
    value_clips = values.reshape(CLIPS, CLIP, D)
    attn, log_total = lax.map(attend_clip, (query_clips, key_clips, value_clips))
    hidden_sum = resid.astype(jnp.float32).reshape(CLIPS, CLIP, D) + attn.astype(jnp.float32)
    inv_rms = lax.rsqrt(lax.optimization_barrier(jnp.mean(hidden_sum * hidden_sum, axis=-1, keepdims=True)) + NORM_EPSILON)
    normed = hidden_sum * inv_rms
    lift_gain = 1.0 + mod_scale[:, None, :]
    normed_mod = (normed * lift_gain + mod_shift[:, None, :]).astype(jnp.bfloat16).reshape(TOKENS, D)
    logits = jnp.dot(normed_mod, router, preferred_element_type=jnp.float32)
    expert_range = jnp.arange(EXPERTS, dtype=jnp.int32)
    first_hot = (expert_ids[:, 0:1] == expert_range[None, :]).astype(jnp.float32)
    second_hot = (expert_ids[:, 1:2] == expert_range[None, :]).astype(jnp.float32)
    margin = lax.optimization_barrier(jnp.sum(logits * first_hot, axis=-1)) - lax.optimization_barrier(jnp.sum(logits * second_hot, axis=-1))
    gate_one = jax.nn.sigmoid(margin)
    gate_two = 1.0 - gate_one
    both_hot = (first_hot + second_hot).reshape(TOKENS // TOK_DEV, TOK_DEV, EXPERTS)
    earlier = (jnp.cumsum(both_hot, axis=1) - both_hot).reshape(TOKENS, EXPERTS)
    token_index = jnp.arange(TOKENS, dtype=jnp.int32)
    device_index = token_index // TOK_DEV
    place_one = device_index * CAP + lax.optimization_barrier(jnp.sum(earlier * first_hot, axis=-1)).astype(jnp.int32)
    place_two = device_index * CAP + lax.optimization_barrier(jnp.sum(earlier * second_hot, axis=-1)).astype(jnp.int32)
    rows_all = TOKENS // TOK_DEV * CAP
    slot_table = jnp.full((EXPERTS, rows_all), 2 * TOKENS, dtype=jnp.int32)
    slot_table = slot_table.at[expert_ids[:, 0], place_one].set(2 * token_index)
    slot_table = slot_table.at[expert_ids[:, 1], place_two].set(2 * token_index + 1)
    padded_in = jnp.concatenate([normed_mod, jnp.zeros((1, D), jnp.bfloat16)], axis=0)

    def expert_forward(expert_item):
        row_index, weight_in, weight_out = expert_item
        rows_in = padded_in[row_index // 2]
        pre_act = jnp.dot(rows_in, weight_in, preferred_element_type=jnp.float32)
        activated = jax.nn.gelu(pre_act).astype(jnp.bfloat16)
        blocks = jnp.einsum('rbf,bfd->brd', activated.astype(jnp.float32).reshape(rows_all, N_CTX, FF_BLOCK), weight_out.astype(jnp.float32).reshape(N_CTX, FF_BLOCK, D))
        return lax.optimization_barrier(jnp.sum(rounded(blocks), axis=0)).astype(jnp.bfloat16)
    expert_rows = lax.map(expert_forward, (slot_table, w_in, w_out))
    result_one = expert_rows[expert_ids[:, 0], place_one].astype(jnp.float32)
    result_two = expert_rows[expert_ids[:, 1], place_two].astype(jnp.float32)
    branch = gate_one[:, None] * result_one + gate_two[:, None] * result_two
    hidden_flat = hidden_sum.reshape(TOKENS, D)
    gated_branch = (mod_gate[:, None, :] * branch.reshape(CLIPS, CLIP, D)).reshape(TOKENS, D)
    mixed_out = (hidden_flat + gated_branch).astype(jnp.bfloat16)
    grad_float = grad_out.astype(jnp.float32)
    branch_grad = (mod_gate[:, None, :] * grad_float.reshape(CLIPS, CLIP, D)).reshape(TOKENS, D)
    grad_one = (gate_one[:, None] * branch_grad).astype(jnp.bfloat16)
    grad_two = (gate_two[:, None] * branch_grad).astype(jnp.bfloat16)
    gate_tilt = (lax.optimization_barrier(jnp.sum(branch_grad * result_one, axis=-1)) - lax.optimization_barrier(jnp.sum(branch_grad * result_two, axis=-1))) * gate_one * gate_two
    logit_grad = (gate_tilt[:, None] * (first_hot - second_hot)).astype(jnp.bfloat16)
    grad_router = jnp.dot(normed_mod.T, logit_grad, preferred_element_type=jnp.float32)
    back_router = jnp.dot(logit_grad, router.T, preferred_element_type=jnp.float32)
    pair_grads = jnp.stack([grad_one, grad_two], axis=1).reshape(2 * TOKENS, D)
    padded_grad = jnp.concatenate([pair_grads, jnp.zeros((1, D), jnp.bfloat16)], axis=0)

    def expert_backward(expert_item):
        row_index, weight_in, weight_out = expert_item
        rows_in = padded_in[row_index // 2]
        rows_grad = padded_grad[row_index]
        pre_act = jnp.dot(rows_in, weight_in, preferred_element_type=jnp.float32)
        activated = jax.nn.gelu(pre_act).astype(jnp.bfloat16)
        act_grad = jnp.dot(rows_grad, weight_out.T, preferred_element_type=jnp.float32)
        gelu_pull = jax.vjp(jax.nn.gelu, pre_act)[1]
        pre_grad = gelu_pull(act_grad)[0].astype(jnp.bfloat16)
        grad_in_weight = jnp.dot(rows_in.T, pre_grad, preferred_element_type=jnp.float32).astype(jnp.bfloat16)
        grad_out_weight = jnp.dot(activated.T, rows_grad, preferred_element_type=jnp.float32).astype(jnp.bfloat16)
        blocks = jnp.einsum('rbf,dbf->brd', pre_grad.astype(jnp.float32).reshape(rows_all, N_CTX, FF_BLOCK), weight_in.astype(jnp.float32).reshape(D, N_CTX, FF_BLOCK))
        return (lax.optimization_barrier(jnp.sum(rounded(blocks), axis=0)).astype(jnp.bfloat16), grad_in_weight, grad_out_weight)
    input_rows, grad_w_in, grad_w_out = lax.map(expert_backward, (slot_table, w_in, w_out))
    input_grad = input_rows[expert_ids[:, 0], place_one].astype(jnp.float32) + input_rows[expert_ids[:, 1], place_two].astype(jnp.float32) + back_router
    lifted = input_grad.reshape(CLIPS, CLIP, D) * lift_gain
    resid_grad = grad_float.reshape(CLIPS, CLIP, D) + inv_rms * (lifted - normed * lax.optimization_barrier(jnp.mean(lifted * normed, axis=-1, keepdims=True)))
    resid_grad = resid_grad.astype(jnp.bfloat16)
    grad_queries, grad_keys, grad_values = lax.map(attend_back, (query_clips, key_clips, value_clips, attn, log_total, resid_grad))
    return (mixed_out, resid_grad.reshape(TOKENS, D), grad_queries.reshape(TOKENS, D), grad_keys.reshape(TOKENS, D), grad_values.reshape(TOKENS, D), grad_w_in, grad_w_out, grad_router)
```

```python
import math

import jax
import jax.numpy as jnp
from jax import lax
from jax.sharding import PartitionSpec as P

HEADS = 16
CORES = 2
LANES = 128
NORM_EPSILON = 1e-06


def rounded(value):
    return lax.optimization_barrier(value.astype(jnp.bfloat16)).astype(jnp.float32)


def dot(left_side, right_side):
    return jnp.dot(left_side, right_side, preferred_element_type=jnp.float32)


def contract_rows(left_side, right_side):
    return lax.dot_general(
        left_side, right_side, (((0,), (0,)), ((), ())), preferred_element_type=jnp.float32
    )


def contract_cols(left_side, right_side):
    return lax.dot_general(
        left_side, right_side, (((1,), (1,)), ((), ())), preferred_element_type=jnp.float32
    )


def swap_core(value):
    size = lax.axis_size("ctx")
    return lax.ppermute(value, "ctx", [(i, i ^ 1) for i in range(size)])


def shift_chip(value, step):
    size = lax.axis_size("ctx")
    chips = size // CORES
    return lax.ppermute(
        value,
        "ctx",
        [(i, ((i // CORES + step) % chips) * CORES + i % CORES) for i in range(size)],
    )


def gather_ctx(value):
    chips = lax.axis_size("ctx") // CORES
    far = [shift_chip(value, step) for step in range(1, chips)]
    blocks = [value, swap_core(value)]
    for block in far:
        blocks += [block, swap_core(block)]
    return blocks


def scatter_ctx(terms):
    chips = lax.axis_size("ctx") // CORES
    sums = []
    order = list(range(1, chips)) + [0]
    for i in order:
        got = swap_core(terms[2 * i + 1].astype(jnp.bfloat16))
        sums.append(terms[2 * i] + got.astype(jnp.float32))
    total = sums[-1]
    for i, part in zip(order[:-1], sums[:-1]):
        total = total + shift_chip(part.astype(jnp.bfloat16), chips - i).astype(jnp.float32)
    return total


def send_expert(blocks, sign):
    size = lax.axis_size("expert")
    out = [blocks[0]]
    for d in range(1, size):
        out.append(
            lax.ppermute(blocks[d], "expert", [(i, (i + sign * d) % size) for i in range(size)])
        )
    return jnp.stack(out)


def local(
    resid,
    queries,
    keys,
    values,
    mod_scale,
    mod_shift,
    mod_gate,
    router,
    w_in,
    w_out,
    expert_ids,
    grad_out,
):
    tok_rows, width = resid.shape
    head_size = width // HEADS
    score_scale = 1.0 / math.sqrt(head_size)
    experts = router.shape[1]
    capacity = 5 * tok_rows // (2 * experts)
    here = lax.axis_index("expert")
    expert_range = jnp.arange(experts, dtype=jnp.int32)

    first_hot = (expert_ids[:, 0:1] == expert_range[None, :]).astype(jnp.float32)
    second_hot = (expert_ids[:, 1:2] == expert_range[None, :]).astype(jnp.float32)
    both_hot = first_hot + second_hot
    earlier = jnp.cumsum(both_hot, axis=0) - both_hot
    ahead = lax.rem(expert_ids - here + experts, experts) * capacity
    place_one = ahead[:, 0] + jnp.sum(earlier * first_hot, axis=-1).astype(jnp.int32)
    place_two = ahead[:, 1] + jnp.sum(earlier * second_hot, axis=-1).astype(jnp.int32)
    slot_range = jnp.arange(experts * capacity, dtype=jnp.int32)
    pick_one = (place_one[:, None] == slot_range[None, :]).astype(jnp.bfloat16)
    pick_two = (place_two[:, None] == slot_range[None, :]).astype(jnp.bfloat16)
    pick_both = pick_one + pick_two

    other_ids = contract_rows(
        pick_one, jnp.broadcast_to(expert_ids[:, 1:2], (tok_rows, LANES)).astype(jnp.bfloat16)
    ) + contract_rows(
        pick_two, jnp.broadcast_to(expert_ids[:, 0:1], (tok_rows, LANES)).astype(jnp.bfloat16)
    )
    grad_rows = jnp.concatenate(
        [
            contract_rows(pick_both, grad_out).astype(jnp.bfloat16),
            other_ids.astype(jnp.bfloat16),
        ],
        axis=1,
    ).reshape(experts, capacity, width + LANES)

    key_blocks = gather_ctx(keys)
    value_blocks = gather_ctx(values)
    arrived_grads = send_expert(grad_rows, 1)
    all_gates = lax.all_gather(mod_gate, "expert", axis=0, tiled=True)

    clip_keys = jnp.concatenate(key_blocks, axis=0)
    clip_values = jnp.concatenate(value_blocks, axis=0)
    clip_len = clip_keys.shape[0]
    query_heads = queries.reshape(tok_rows, HEADS, head_size)
    key_heads = clip_keys.reshape(clip_len, HEADS, head_size)
    value_heads = clip_values.reshape(clip_len, HEADS, head_size)

    w_in_own, w_out_own, queries_own, _ = lax.optimization_barrier(
        (w_in[0], w_out[0], queries, (clip_keys, clip_values))
    )
    in_blocks = gather_ctx(w_in_own)
    out_blocks = gather_ctx(w_out_own)

    scores = (
        jnp.einsum("qhd,khd->hqk", query_heads, key_heads, preferred_element_type=jnp.float32)
        * score_scale
    )
    row_top = jnp.max(scores, axis=-1)
    exp_scores = jnp.exp(scores - row_top[..., None])
    row_total = jnp.sum(exp_scores, axis=-1)
    mixed_values = jnp.einsum(
        "hqk,khd->qhd",
        exp_scores.astype(jnp.bfloat16),
        value_heads,
        preferred_element_type=jnp.float32,
    )
    attn_heads = (mixed_values / row_total.T[:, :, None]).astype(jnp.bfloat16)
    log_total = row_top + jnp.log(row_total)
    hidden_sum = resid.astype(jnp.float32) + attn_heads.reshape(tok_rows, width).astype(jnp.float32)
    inv_rms = lax.rsqrt(jnp.mean(hidden_sum * hidden_sum, axis=-1, keepdims=True) + NORM_EPSILON)
    normed = hidden_sum * inv_rms
    lift_gain = 1.0 + mod_scale
    normed_mod = (normed * lift_gain + mod_shift).astype(jnp.bfloat16)
    sent_rows = (
        contract_rows(pick_both, normed_mod)
        .astype(jnp.bfloat16)
        .reshape(experts, capacity, width)
    )
    rows_flat = send_expert(sent_rows, 1).reshape(-1, width)

    query_blocks = gather_ctx(queries_own)
    total_blocks = gather_ctx(log_total)

    logits = dot(normed_mod, router)
    margin = jnp.sum(logits * first_hot, axis=-1) - jnp.sum(logits * second_hot, axis=-1)
    gate_one = jax.nn.sigmoid(margin)
    gate_two = 1.0 - gate_one

    pre_acts = [dot(rows_flat, block) for block in in_blocks]
    activated = [jax.nn.gelu(pre).astype(jnp.bfloat16) for pre in pre_acts]
    block_sum = 0.0
    for act, block in zip(activated, out_blocks):
        block_sum = block_sum + rounded(dot(act, block))
    expert_y = block_sum.astype(jnp.bfloat16)

    slot_grads = arrived_grads.reshape(-1, width + LANES)
    other = slot_grads[:, width : width + 1].astype(jnp.int32)
    slot_logits = dot(rows_flat, router)
    slot_margin = jnp.sum(
        slot_logits
        * (
            (expert_range[None, :] == here).astype(jnp.float32)
            - (expert_range[None, :] == other).astype(jnp.float32)
        ),
        axis=-1,
        keepdims=True,
    )
    slot_gate = jax.nn.sigmoid(slot_margin)
    source = lax.rem(here - expert_range + experts, experts)
    source_hot = (source[:, None] == expert_range[None, :]).astype(jnp.float32)
    source_gates = jnp.sum(source_hot[:, :, None] * all_gates[None, :, :], axis=1)
    branch_rows = (
        source_gates[:, None, :]
        * slot_grads[:, :width].reshape(experts, capacity, width).astype(jnp.float32)
    ).reshape(-1, width)
    y_grad = (slot_gate * branch_rows).astype(jnp.bfloat16)
    pre_grads = [
        jax.vjp(jax.nn.gelu, pre)[1](contract_cols(y_grad, block))[0].astype(jnp.bfloat16)
        for pre, block in zip(pre_acts, out_blocks)
    ]
    block_sum = 0.0
    for pre_grad, block in zip(pre_grads, in_blocks):
        block_sum = block_sum + rounded(contract_cols(pre_grad, block))
    slot_dot = jnp.sum(branch_rows * expert_y.astype(jnp.float32), axis=-1, keepdims=True)
    high = rounded(slot_dot)
    middle = rounded(slot_dot - high)
    low = slot_dot - high - middle
    lane = jnp.arange(LANES, dtype=jnp.int32)[None, :]
    pieces = jnp.where(lane == 0, high, jnp.where(lane == 1, middle, jnp.where(lane == 2, low, 0.0)))
    back_rows = send_expert(
        jnp.concatenate(
            [block_sum.astype(jnp.bfloat16), pieces.astype(jnp.bfloat16)], axis=1
        ).reshape(experts, capacity, width + LANES),
        -1,
    )
    returned_y, _ = lax.optimization_barrier((expert_y, block_sum))
    returned = send_expert(returned_y.reshape(experts, capacity, width), -1)

    grad_w_in = scatter_ctx([contract_rows(rows_flat, pre_grad) for pre_grad in pre_grads])
    grad_w_out = scatter_ctx([contract_rows(act, y_grad) for act in activated])
    grad_w_in = grad_w_in.astype(jnp.bfloat16)[None]
    grad_w_out = grad_w_out.astype(jnp.bfloat16)[None]

    grad_float = grad_out.astype(jnp.float32)
    back_flat = back_rows.reshape(experts * capacity, width + LANES)
    parts = back_flat[:, width:]
    dots = jnp.sum(dot(pick_one, parts), axis=-1) - jnp.sum(dot(pick_two, parts), axis=-1)
    gate_tilt = dots * gate_one * gate_two
    logit_grad = (gate_tilt[:, None] * (first_hot - second_hot)).astype(jnp.bfloat16)
    back_router = contract_cols(logit_grad, router)
    input_grad = dot(pick_both, back_flat[:, :width]) + back_router
    lifted = input_grad * lift_gain
    resid_grad = grad_float + inv_rms * (
        lifted - normed * jnp.mean(lifted * normed, axis=-1, keepdims=True)
    )
    resid_grad = resid_grad.astype(jnp.bfloat16)
    grad_heads = resid_grad.reshape(tok_rows, HEADS, head_size)
    row_dot = jnp.einsum("qhd,qhd->hq", grad_heads, attn_heads, preferred_element_type=jnp.float32)
    grad_blocks = gather_ctx(resid_grad)
    dot_blocks = gather_ctx(row_dot)

    router_term = contract_rows(logit_grad, normed_mod)
    router_term = lax.optimization_barrier(router_term.reshape(-1, LANES))
    router_sum = lax.optimization_barrier(lax.psum(router_term, ("expert", "ctx")))
    grad_router = router_sum.reshape(experts, width).T

    prob = jnp.exp(scores - log_total[..., None])
    value_pull = jnp.einsum(
        "qhd,khd->hqk", grad_heads, value_heads, preferred_element_type=jnp.float32
    )
    score_grad = (prob * (value_pull - row_dot[..., None])).astype(jnp.bfloat16)
    grad_queries = (
        (
            jnp.einsum("hqk,khd->qhd", score_grad, key_heads, preferred_element_type=jnp.float32)
            * score_scale
        )
        .astype(jnp.bfloat16)
        .reshape(tok_rows, width)
    )

    own_keys = keys.reshape(tok_rows, HEADS, head_size)
    own_values = values.reshape(tok_rows, HEADS, head_size)
    grad_keys = 0.0
    grad_values = 0.0
    for query_block, total_block, grad_block, dot_block in zip(
        query_blocks, total_blocks, grad_blocks, dot_blocks
    ):
        block_queries = query_block.reshape(tok_rows, HEADS, head_size)
        block_grads = grad_block.reshape(tok_rows, HEADS, head_size)
        block_scores = (
            jnp.einsum("qhd,khd->hqk", block_queries, own_keys, preferred_element_type=jnp.float32)
            * score_scale
        )
        block_prob = jnp.exp(block_scores - total_block[..., None])
        block_pull = jnp.einsum(
            "qhd,khd->hqk", block_grads, own_values, preferred_element_type=jnp.float32
        )
        block_score_grad = (block_prob * (block_pull - dot_block[..., None])).astype(jnp.bfloat16)
        grad_keys = grad_keys + (
            jnp.einsum(
                "hqk,qhd->khd", block_score_grad, block_queries, preferred_element_type=jnp.float32
            )
            * score_scale
        )
        grad_values = grad_values + jnp.einsum(
            "hqk,qhd->khd",
            block_prob.astype(jnp.bfloat16),
            block_grads,
            preferred_element_type=jnp.float32,
        )
    grad_keys = grad_keys.astype(jnp.bfloat16).reshape(tok_rows, width)
    grad_values = grad_values.astype(jnp.bfloat16).reshape(tok_rows, width)

    home_flat = returned.reshape(experts * capacity, width)
    branch = gate_one[:, None] * dot(pick_one, home_flat) + gate_two[:, None] * dot(
        pick_two, home_flat
    )
    mixed_out = (hidden_sum + mod_gate * branch).astype(jnp.bfloat16)
    return (
        mixed_out,
        resid_grad,
        grad_queries,
        grad_keys,
        grad_values,
        grad_w_in,
        grad_w_out,
        grad_router,
    )


def solution(mesh):
    return jax.shard_map(
        local,
        mesh=mesh,
        in_specs=(
            P(("expert", "ctx"), None),
            P(("expert", "ctx"), None),
            P(("expert", "ctx"), None),
            P(("expert", "ctx"), None),
            P("expert", None),
            P("expert", None),
            P("expert", None),
            P(),
            P("expert", None, "ctx"),
            P("expert", "ctx", None),
            P(("expert", "ctx"), None),
            P(("expert", "ctx"), None),
        ),
        out_specs=(
            P(("expert", "ctx"), None),
            P(("expert", "ctx"), None),
            P(("expert", "ctx"), None),
            P(("expert", "ctx"), None),
            P(("expert", "ctx"), None),
            P("expert", None, "ctx"),
            P("expert", "ctx", None),
            P(),
        ),
        check_vma=False,
    )
```

```python
import math

import jax
import jax.numpy as jnp
from jax import lax
from jax.sharding import PartitionSpec as P

HEADS = 16
CORES = 2
LANES = 128
NORM_EPSILON = 1e-06


def rounded(value):
    return lax.optimization_barrier(value.astype(jnp.bfloat16)).astype(jnp.float32)


def dot(left_side, right_side):
    return jnp.dot(left_side, right_side, preferred_element_type=jnp.float32)


def contract_rows(left_side, right_side):
    return lax.dot_general(
        left_side, right_side, (((0,), (0,)), ((), ())), preferred_element_type=jnp.float32
    )


def contract_cols(left_side, right_side):
    return lax.dot_general(
        left_side, right_side, (((1,), (1,)), ((), ())), preferred_element_type=jnp.float32
    )


def swap_core(value):
    size = lax.axis_size("ctx")
    return lax.ppermute(value, "ctx", [(i, i ^ 1) for i in range(size)])


def shift_chip(value, step):
    size = lax.axis_size("ctx")
    chips = size // CORES
    return lax.ppermute(
        value,
        "ctx",
        [(i, ((i // CORES + step) % chips) * CORES + i % CORES) for i in range(size)],
    )


def gather_ctx(value):
    chips = lax.axis_size("ctx") // CORES
    far = [shift_chip(value, step) for step in range(1, chips)]
    blocks = [value, swap_core(value)]
    for block in far:
        blocks += [block, swap_core(block)]
    return blocks


def pair_sums(terms):
    chips = lax.axis_size("ctx") // CORES
    far = []
    for i in range(1, chips):
        got = swap_core(terms[2 * i + 1].astype(jnp.bfloat16))
        far.append((terms[2 * i] + got.astype(jnp.float32)).astype(jnp.bfloat16))
    return far, terms[0], swap_core(terms[1].astype(jnp.bfloat16))


def chip_sums(far, own, got):
    chips = lax.axis_size("ctx") // CORES
    total = own + got.astype(jnp.float32)
    for i, part in enumerate(far, 1):
        total = total + shift_chip(part, chips - i).astype(jnp.float32)
    return total


def send_expert(blocks, sign):
    size = lax.axis_size("expert")
    out = [blocks[0]]
    for d in range(1, size):
        out.append(
            lax.ppermute(blocks[d], "expert", [(i, (i + sign * d) % size) for i in range(size)])
        )
    return jnp.stack(out)


def swap_with(value, axis, step):
    size = lax.axis_size(axis)
    return lax.ppermute(value, axis, [(i, i ^ step) for i in range(size)])


def doubled_sum(value):
    for axis in ("ctx", "expert"):
        step = 1
        while step < lax.axis_size(axis):
            value = value + swap_with(value, axis, step)
            step *= 2
    return value


def doubled_gather(value):
    step = 1
    while step < lax.axis_size("expert"):
        value = jnp.concatenate([value, swap_with(value, "expert", step)], axis=0)
        step *= 2
    return value


def local(
    resid,
    queries,
    keys,
    values,
    mod_scale,
    mod_shift,
    mod_gate,
    router,
    w_in,
    w_out,
    expert_ids,
    grad_out,
):
    tok_rows, width = resid.shape
    head_size = width // HEADS
    score_scale = 1.0 / math.sqrt(head_size)
    experts = router.shape[1]
    capacity = 5 * tok_rows // (2 * experts)
    here = lax.axis_index("expert")
    expert_range = jnp.arange(experts, dtype=jnp.int32)

    first_hot = (expert_ids[:, 0:1] == expert_range[None, :]).astype(jnp.float32)
    second_hot = (expert_ids[:, 1:2] == expert_range[None, :]).astype(jnp.float32)
    both_hot = first_hot + second_hot
    earlier = jnp.cumsum(both_hot, axis=0) - both_hot
    ahead = lax.rem(expert_ids - here + experts, experts) * capacity
    place_one = ahead[:, 0] + jnp.sum(earlier * first_hot, axis=-1).astype(jnp.int32)
    place_two = ahead[:, 1] + jnp.sum(earlier * second_hot, axis=-1).astype(jnp.int32)
    slot_range = jnp.arange(experts * capacity, dtype=jnp.int32)
    pick_one = (place_one[:, None] == slot_range[None, :]).astype(jnp.bfloat16)
    pick_two = (place_two[:, None] == slot_range[None, :]).astype(jnp.bfloat16)
    pick_both = pick_one + pick_two

    other_ids = contract_rows(
        pick_one, jnp.broadcast_to(expert_ids[:, 1:2], (tok_rows, LANES)).astype(jnp.bfloat16)
    ) + contract_rows(
        pick_two, jnp.broadcast_to(expert_ids[:, 0:1], (tok_rows, LANES)).astype(jnp.bfloat16)
    )
    grad_rows = jnp.concatenate(
        [
            contract_rows(pick_both, grad_out).astype(jnp.bfloat16),
            other_ids.astype(jnp.bfloat16),
        ],
        axis=1,
    ).reshape(experts, capacity, width + LANES)

    key_blocks = gather_ctx(keys)
    value_blocks = gather_ctx(values)
    arrived_grads = send_expert(grad_rows, 1)
    all_gates = doubled_gather(mod_gate)

    clip_keys = jnp.concatenate(key_blocks, axis=0)
    clip_values = jnp.concatenate(value_blocks, axis=0)
    clip_len = clip_keys.shape[0]
    query_heads = queries.reshape(tok_rows, HEADS, head_size)
    key_heads = clip_keys.reshape(clip_len, HEADS, head_size)
    value_heads = clip_values.reshape(clip_len, HEADS, head_size)

    w_in_own, w_out_own, queries_own, _ = lax.optimization_barrier(
        (w_in[0], w_out[0], queries, (clip_keys, clip_values))
    )
    in_blocks = gather_ctx(w_in_own)
    out_blocks = gather_ctx(w_out_own)

    scores = (
        jnp.einsum("qhd,khd->hqk", query_heads, key_heads, preferred_element_type=jnp.float32)
        * score_scale
    )
    row_top = jnp.max(scores, axis=-1)
    exp_scores = jnp.exp(scores - row_top[..., None])
    row_total = jnp.sum(exp_scores, axis=-1)
    mixed_values = jnp.einsum(
        "hqk,khd->qhd",
        exp_scores.astype(jnp.bfloat16),
        value_heads,
        preferred_element_type=jnp.float32,
    )
    attn_heads = (mixed_values / row_total.T[:, :, None]).astype(jnp.bfloat16)
    log_total = row_top + jnp.log(row_total)
    hidden_sum = resid.astype(jnp.float32) + attn_heads.reshape(tok_rows, width).astype(jnp.float32)
    inv_rms = lax.rsqrt(jnp.mean(hidden_sum * hidden_sum, axis=-1, keepdims=True) + NORM_EPSILON)
    normed = hidden_sum * inv_rms
    lift_gain = 1.0 + mod_scale
    normed_mod = (normed * lift_gain + mod_shift).astype(jnp.bfloat16)
    normed_mod, arrived_grads, all_gates = lax.optimization_barrier(
        (normed_mod, arrived_grads, all_gates)
    )
    sent_rows = (
        contract_rows(pick_both, normed_mod)
        .astype(jnp.bfloat16)
        .reshape(experts, capacity, width)
    )
    rows_flat = send_expert(sent_rows, 1).reshape(-1, width)

    query_blocks = gather_ctx(queries_own)
    total_blocks = gather_ctx(log_total)

    logits = dot(normed_mod, router)
    margin = jnp.sum(logits * first_hot, axis=-1) - jnp.sum(logits * second_hot, axis=-1)
    gate_one = jax.nn.sigmoid(margin)
    gate_two = 1.0 - gate_one

    pre_acts = [dot(rows_flat, block) for block in in_blocks]
    activated = [jax.nn.gelu(pre).astype(jnp.bfloat16) for pre in pre_acts]
    block_sum = 0.0
    for act, block in zip(activated, out_blocks):
        block_sum = block_sum + rounded(dot(act, block))
    expert_y = block_sum.astype(jnp.bfloat16)

    slot_grads = arrived_grads.reshape(-1, width + LANES)
    other = slot_grads[:, width : width + 1].astype(jnp.int32)
    slot_logits = dot(rows_flat, router)
    slot_margin = jnp.sum(
        slot_logits
        * (
            (expert_range[None, :] == here).astype(jnp.float32)
            - (expert_range[None, :] == other).astype(jnp.float32)
        ),
        axis=-1,
        keepdims=True,
    )
    slot_gate = jax.nn.sigmoid(slot_margin)
    source = lax.rem(here - expert_range + experts, experts)
    source_hot = ((source ^ here)[:, None] == expert_range[None, :]).astype(jnp.float32)
    source_gates = jnp.sum(source_hot[:, :, None] * all_gates[None, :, :], axis=1)
    branch_rows = (
        source_gates[:, None, :]
        * slot_grads[:, :width].reshape(experts, capacity, width).astype(jnp.float32)
    ).reshape(-1, width)
    y_grad = (slot_gate * branch_rows).astype(jnp.bfloat16)
    pre_grads = [
        jax.vjp(jax.nn.gelu, pre)[1](contract_cols(y_grad, block))[0].astype(jnp.bfloat16)
        for pre, block in zip(pre_acts, out_blocks)
    ]
    block_sum = 0.0
    for pre_grad, block in zip(pre_grads, in_blocks):
        block_sum = block_sum + rounded(contract_cols(pre_grad, block))
    slot_dot = jnp.sum(branch_rows * expert_y.astype(jnp.float32), axis=-1, keepdims=True)
    high = rounded(slot_dot)
    middle = rounded(slot_dot - high)
    low = slot_dot - high - middle
    lane = jnp.arange(LANES, dtype=jnp.int32)[None, :]
    pieces = jnp.where(lane == 0, high, jnp.where(lane == 1, middle, jnp.where(lane == 2, low, 0.0)))
    back_rows = send_expert(
        jnp.concatenate(
            [block_sum.astype(jnp.bfloat16), pieces.astype(jnp.bfloat16)], axis=1
        ).reshape(experts, capacity, width + LANES),
        -1,
    )
    rows_flat, y_grad, pre_grads, activated, _ = lax.optimization_barrier(
        (rows_flat, y_grad, pre_grads, activated, block_sum)
    )
    in_sums = pair_sums([contract_rows(rows_flat, pre_grad) for pre_grad in pre_grads])
    out_sums = pair_sums([contract_rows(act, y_grad) for act in activated])

    back_rows, returned_y, in_far, out_far = lax.optimization_barrier(
        (back_rows, expert_y, in_sums[0], out_sums[0])
    )
    grad_w_in = chip_sums(in_far, *in_sums[1:]).astype(jnp.bfloat16)[None]
    grad_w_out = chip_sums(out_far, *out_sums[1:]).astype(jnp.bfloat16)[None]
    returned = send_expert(returned_y.reshape(experts, capacity, width), -1)
    grad_float = grad_out.astype(jnp.float32)
    back_flat = back_rows.reshape(experts * capacity, width + LANES)
    parts = back_flat[:, width:]
    dots = jnp.sum(dot(pick_one, parts), axis=-1) - jnp.sum(dot(pick_two, parts), axis=-1)
    gate_tilt = dots * gate_one * gate_two
    logit_grad = (gate_tilt[:, None] * (first_hot - second_hot)).astype(jnp.bfloat16)
    back_router = contract_cols(logit_grad, router)
    input_grad = dot(pick_both, back_flat[:, :width]) + back_router
    lifted = input_grad * lift_gain
    resid_grad = grad_float + inv_rms * (
        lifted - normed * jnp.mean(lifted * normed, axis=-1, keepdims=True)
    )
    resid_grad = resid_grad.astype(jnp.bfloat16)
    grad_heads = resid_grad.reshape(tok_rows, HEADS, head_size)
    row_dot = jnp.einsum("qhd,qhd->hq", grad_heads, attn_heads, preferred_element_type=jnp.float32)
    grad_blocks = gather_ctx(resid_grad)
    dot_blocks = gather_ctx(row_dot)

    router_term = contract_rows(logit_grad, normed_mod)
    router_term = lax.optimization_barrier(router_term.reshape(-1, LANES))
    router_sum = lax.optimization_barrier(doubled_sum(router_term))
    grad_router = router_sum.reshape(experts, width).T

    prob = jnp.exp(scores - log_total[..., None])
    value_pull = jnp.einsum(
        "qhd,khd->hqk", grad_heads, value_heads, preferred_element_type=jnp.float32
    )
    score_grad = (prob * (value_pull - row_dot[..., None])).astype(jnp.bfloat16)
    grad_queries = (
        (
            jnp.einsum("hqk,khd->qhd", score_grad, key_heads, preferred_element_type=jnp.float32)
            * score_scale
        )
        .astype(jnp.bfloat16)
        .reshape(tok_rows, width)
    )

    own_keys = keys.reshape(tok_rows, HEADS, head_size)
    own_values = values.reshape(tok_rows, HEADS, head_size)
    grad_keys = 0.0
    grad_values = 0.0
    for query_block, total_block, grad_block, dot_block in zip(
        query_blocks, total_blocks, grad_blocks, dot_blocks
    ):
        block_queries = query_block.reshape(tok_rows, HEADS, head_size)
        block_grads = grad_block.reshape(tok_rows, HEADS, head_size)
        block_scores = (
            jnp.einsum("qhd,khd->hqk", block_queries, own_keys, preferred_element_type=jnp.float32)
            * score_scale
        )
        block_prob = jnp.exp(block_scores - total_block[..., None])
        block_pull = jnp.einsum(
            "qhd,khd->hqk", block_grads, own_values, preferred_element_type=jnp.float32
        )
        block_score_grad = (block_prob * (block_pull - dot_block[..., None])).astype(jnp.bfloat16)
        grad_keys = grad_keys + (
            jnp.einsum(
                "hqk,qhd->khd", block_score_grad, block_queries, preferred_element_type=jnp.float32
            )
            * score_scale
        )
        grad_values = grad_values + jnp.einsum(
            "hqk,qhd->khd",
            block_prob.astype(jnp.bfloat16),
            block_grads,
            preferred_element_type=jnp.float32,
        )
    grad_keys = grad_keys.astype(jnp.bfloat16).reshape(tok_rows, width)
    grad_values = grad_values.astype(jnp.bfloat16).reshape(tok_rows, width)

    home_flat = returned.reshape(experts * capacity, width)
    branch = gate_one[:, None] * dot(pick_one, home_flat) + gate_two[:, None] * dot(
        pick_two, home_flat
    )
    mixed_out = (hidden_sum + mod_gate * branch).astype(jnp.bfloat16)
    return (
        mixed_out,
        resid_grad,
        grad_queries,
        grad_keys,
        grad_values,
        grad_w_in,
        grad_w_out,
        grad_router,
    )


def solution(mesh):
    return jax.shard_map(
        local,
        mesh=mesh,
        in_specs=(
            P(("expert", "ctx"), None),
            P(("expert", "ctx"), None),
            P(("expert", "ctx"), None),
            P(("expert", "ctx"), None),
            P("expert", None),
            P("expert", None),
            P("expert", None),
            P(),
            P("expert", None, "ctx"),
            P("expert", "ctx", None),
            P(("expert", "ctx"), None),
            P(("expert", "ctx"), None),
        ),
        out_specs=(
            P(("expert", "ctx"), None),
            P(("expert", "ctx"), None),
            P(("expert", "ctx"), None),
            P(("expert", "ctx"), None),
            P(("expert", "ctx"), None),
            P("expert", None, "ctx"),
            P("expert", "ctx", None),
            P(),
        ),
        check_vma=False,
    )
```

```python
import math

import jax
import jax.numpy as jnp
from jax import lax
from jax.sharding import PartitionSpec as P


HEADS = 16
CORES = 2
LANES = 128
NORM_EPSILON = 1e-06


def rounded(value):
    return lax.optimization_barrier(value.astype(jnp.bfloat16)).astype(jnp.float32)


def dot(left_side, right_side):
    return jnp.dot(left_side, right_side, preferred_element_type=jnp.float32)


def contract_rows(left_side, right_side):
    return lax.dot_general(
        left_side, right_side, (((0,), (0,)), ((), ())), preferred_element_type=jnp.float32
    )


def contract_cols(left_side, right_side):
    return lax.dot_general(
        left_side, right_side, (((1,), (1,)), ((), ())), preferred_element_type=jnp.float32
    )


def swap_core(value):
    size = lax.axis_size("ctx")
    return lax.ppermute(value, "ctx", [(i, i ^ 1) for i in range(size)])


def shift_chip(value, step):
    size = lax.axis_size("ctx")
    chips = size // CORES
    return lax.ppermute(
        value,
        "ctx",
        [(i, ((i // CORES + step) % chips) * CORES + i % CORES) for i in range(size)],
    )


def gather_ctx(value):
    chips = lax.axis_size("ctx") // CORES
    far = [shift_chip(value, step) for step in range(1, chips)]
    blocks = [value, swap_core(value)]
    for block in far:
        blocks += [block, swap_core(block)]
    return blocks


def pair_sums(terms):
    chips = lax.axis_size("ctx") // CORES
    far = []
    for i in range(1, chips):
        got = swap_core(terms[2 * i + 1].astype(jnp.bfloat16))
        far.append((terms[2 * i] + got.astype(jnp.float32)).astype(jnp.bfloat16))
    return far, terms[0], swap_core(terms[1].astype(jnp.bfloat16))


def chip_sums(far, own, got):
    chips = lax.axis_size("ctx") // CORES
    total = own + got.astype(jnp.float32)
    for i, part in enumerate(far, 1):
        got = shift_chip(part, chips - i)
        total = total + got.astype(jnp.float32)
    return total


def send_expert(blocks, sign):
    size = lax.axis_size("expert")
    out = [blocks[0]]
    for d in range(1, size):
        out.append(
            lax.ppermute(blocks[d], "expert", [(i, (i + sign * d) % size) for i in range(size)])
        )
    return jnp.stack(out)


def swap_with(value, axis, step):
    size = lax.axis_size(axis)
    return lax.ppermute(value, axis, [(i, i ^ step) for i in range(size)])


def doubled_sum(value):
    steps = [("ctx", 1)]
    for axis, step in (("expert", 1), ("ctx", CORES)):
        while step < lax.axis_size(axis):
            steps.append((axis, step))
            step *= 2
    for axis, step in steps:
        got = swap_with(value, axis, step)
        value = value + got
    return value


def doubled_gather(value):
    step = 1
    while step < lax.axis_size("expert"):
        value = jnp.concatenate([value, swap_with(value, "expert", step)], axis=0)
        step *= 2
    return value


def local(
    resid,
    queries,
    keys,
    values,
    mod_scale,
    mod_shift,
    mod_gate,
    router,
    w_in,
    w_out,
    expert_ids,
    grad_out,
):
    tok_rows, width = resid.shape
    head_size = width // HEADS
    score_scale = 1.0 / math.sqrt(head_size)
    experts = router.shape[1]
    capacity = 5 * tok_rows // (2 * experts)
    here = lax.axis_index("expert")
    expert_range = jnp.arange(experts, dtype=jnp.int32)

    first_hot = (expert_ids[:, 0:1] == expert_range[None, :]).astype(jnp.float32)
    second_hot = (expert_ids[:, 1:2] == expert_range[None, :]).astype(jnp.float32)
    both_hot = first_hot + second_hot
    earlier = jnp.cumsum(both_hot, axis=0) - both_hot
    ahead = lax.rem(expert_ids - here + experts, experts) * capacity
    place_one = ahead[:, 0] + jnp.sum(earlier * first_hot, axis=-1).astype(jnp.int32)
    place_two = ahead[:, 1] + jnp.sum(earlier * second_hot, axis=-1).astype(jnp.int32)
    slot_range = jnp.arange(experts * capacity, dtype=jnp.int32)
    pick_one = (place_one[:, None] == slot_range[None, :]).astype(jnp.bfloat16)
    pick_two = (place_two[:, None] == slot_range[None, :]).astype(jnp.bfloat16)
    pick_both = pick_one + pick_two

    other_ids = contract_rows(
        pick_one, jnp.broadcast_to(expert_ids[:, 1:2], (tok_rows, LANES)).astype(jnp.bfloat16)
    ) + contract_rows(
        pick_two, jnp.broadcast_to(expert_ids[:, 0:1], (tok_rows, LANES)).astype(jnp.bfloat16)
    )
    grad_rows = jnp.concatenate(
        [
            contract_rows(pick_both, grad_out).astype(jnp.bfloat16),
            other_ids.astype(jnp.bfloat16),
        ],
        axis=1,
    ).reshape(experts, capacity, width + LANES)

    key_blocks = gather_ctx(keys)
    value_blocks = gather_ctx(values)
    all_gates = doubled_gather(mod_gate)
    grad_rows, all_gates = lax.optimization_barrier((grad_rows, all_gates))
    arrived_grads = send_expert(grad_rows, 1)

    clip_keys = jnp.concatenate(key_blocks, axis=0)
    clip_values = jnp.concatenate(value_blocks, axis=0)
    clip_len = clip_keys.shape[0]
    query_heads = queries.reshape(tok_rows, HEADS, head_size)
    key_heads = clip_keys.reshape(clip_len, HEADS, head_size)
    value_heads = clip_values.reshape(clip_len, HEADS, head_size)

    w_in_own, w_out_own, queries_own, _ = lax.optimization_barrier(
        (w_in[0], w_out[0], queries, (clip_keys, clip_values))
    )
    in_blocks = gather_ctx(w_in_own)
    out_blocks = gather_ctx(w_out_own)

    scores = (
        jnp.einsum("qhd,khd->hqk", query_heads, key_heads, preferred_element_type=jnp.float32)
        * score_scale
    )
    row_top = jnp.max(scores, axis=-1)
    exp_scores = jnp.exp(scores - row_top[..., None])
    row_total = jnp.sum(exp_scores, axis=-1)
    mixed_values = jnp.einsum(
        "hqk,khd->qhd",
        exp_scores.astype(jnp.bfloat16),
        value_heads,
        preferred_element_type=jnp.float32,
    )
    attn_heads = (mixed_values / row_total.T[:, :, None]).astype(jnp.bfloat16)
    log_total = row_top + jnp.log(row_total)
    hidden_sum = resid.astype(jnp.float32) + attn_heads.reshape(tok_rows, width).astype(jnp.float32)
    inv_rms = lax.rsqrt(jnp.mean(hidden_sum * hidden_sum, axis=-1, keepdims=True) + NORM_EPSILON)
    normed = hidden_sum * inv_rms
    lift_gain = 1.0 + mod_scale
    normed_mod = (normed * lift_gain + mod_shift).astype(jnp.bfloat16)
    normed_mod, arrived_grads = lax.optimization_barrier((normed_mod, arrived_grads))
    sent_rows = (
        contract_rows(pick_both, normed_mod)
        .astype(jnp.bfloat16)
        .reshape(experts, capacity, width)
    )
    rows_flat = send_expert(sent_rows, 1).reshape(-1, width)

    query_blocks = gather_ctx(queries_own)
    total_blocks = gather_ctx(log_total)

    logits = dot(normed_mod, router)
    margin = jnp.sum(logits * first_hot, axis=-1) - jnp.sum(logits * second_hot, axis=-1)
    gate_one = jax.nn.sigmoid(margin)
    gate_two = 1.0 - gate_one

    pre_acts = [dot(rows_flat, block) for block in in_blocks]
    activated = [jax.nn.gelu(pre).astype(jnp.bfloat16) for pre in pre_acts]
    block_sum = 0.0
    for act, block in zip(activated, out_blocks):
        block_sum = block_sum + rounded(dot(act, block))
    expert_y = block_sum.astype(jnp.bfloat16)

    slot_grads = arrived_grads.reshape(-1, width + LANES)
    other = slot_grads[:, width : width + 1].astype(jnp.int32)
    slot_logits = dot(rows_flat, router)
    slot_margin = jnp.sum(
        slot_logits
        * (
            (expert_range[None, :] == here).astype(jnp.float32)
            - (expert_range[None, :] == other).astype(jnp.float32)
        ),
        axis=-1,
        keepdims=True,
    )
    slot_gate = jax.nn.sigmoid(slot_margin)
    source = lax.rem(here - expert_range + experts, experts)
    source_hot = ((source ^ here)[:, None] == expert_range[None, :]).astype(jnp.float32)
    source_gates = jnp.sum(source_hot[:, :, None] * all_gates[None, :, :], axis=1)
    branch_rows = (
        source_gates[:, None, :]
        * slot_grads[:, :width].reshape(experts, capacity, width).astype(jnp.float32)
    ).reshape(-1, width)
    y_grad = (slot_gate * branch_rows).astype(jnp.bfloat16)
    pre_grads = [
        jax.vjp(jax.nn.gelu, pre)[1](contract_cols(y_grad, block))[0].astype(jnp.bfloat16)
        for pre, block in zip(pre_acts, out_blocks)
    ]
    block_sum = 0.0
    for pre_grad, block in zip(pre_grads, in_blocks):
        block_sum = block_sum + rounded(contract_cols(pre_grad, block))
    slot_dot = jnp.sum(branch_rows * expert_y.astype(jnp.float32), axis=-1, keepdims=True)
    high = rounded(slot_dot)
    middle = rounded(slot_dot - high)
    low = slot_dot - high - middle
    lane = jnp.arange(LANES, dtype=jnp.int32)[None, :]
    pieces = jnp.where(lane == 0, high, jnp.where(lane == 1, middle, jnp.where(lane == 2, low, 0.0)))
    back_rows = send_expert(
        jnp.concatenate(
            [block_sum.astype(jnp.bfloat16), pieces.astype(jnp.bfloat16)], axis=1
        ).reshape(experts, capacity, width + LANES),
        -1,
    )
    rows_flat, y_grad, pre_grads, activated, _ = lax.optimization_barrier(
        (rows_flat, y_grad, pre_grads, activated, block_sum)
    )
    in_sums = pair_sums([contract_rows(rows_flat, pre_grad) for pre_grad in pre_grads])
    out_sums = pair_sums([contract_rows(act, y_grad) for act in activated])

    back_rows, returned_y, in_far, out_far = lax.optimization_barrier(
        (back_rows, expert_y, in_sums[0], out_sums[0])
    )
    grad_w_in = chip_sums(in_far, *in_sums[1:]).astype(jnp.bfloat16)[None]
    grad_w_out = chip_sums(out_far, *out_sums[1:]).astype(jnp.bfloat16)[None]
    returned = send_expert(returned_y.reshape(experts, capacity, width), -1)
    grad_float = grad_out.astype(jnp.float32)
    back_flat = back_rows.reshape(experts * capacity, width + LANES)
    parts = back_flat[:, width:]
    dots = jnp.sum(dot(pick_one, parts), axis=-1) - jnp.sum(dot(pick_two, parts), axis=-1)
    gate_tilt = dots * gate_one * gate_two
    logit_grad = (gate_tilt[:, None] * (first_hot - second_hot)).astype(jnp.bfloat16)
    back_router = contract_cols(logit_grad, router)
    input_grad = dot(pick_both, back_flat[:, :width])
    input_grad = input_grad + back_router
    lifted = input_grad * lift_gain
    resid_grad = grad_float + inv_rms * (
        lifted - normed * jnp.mean(lifted * normed, axis=-1, keepdims=True)
    )
    resid_grad = resid_grad.astype(jnp.bfloat16)
    grad_heads = resid_grad.reshape(tok_rows, HEADS, head_size)
    row_dot = jnp.einsum("qhd,qhd->hq", grad_heads, attn_heads, preferred_element_type=jnp.float32)
    grad_blocks = gather_ctx(resid_grad)
    dot_blocks = gather_ctx(row_dot)

    router_term = contract_rows(logit_grad, normed_mod)
    router_term = lax.optimization_barrier(router_term.reshape(-1, LANES))
    router_sum = lax.optimization_barrier(doubled_sum(router_term))
    grad_router = router_sum.reshape(experts, width).T

    prob = jnp.exp(scores - log_total[..., None])
    value_pull = jnp.einsum(
        "qhd,khd->hqk", grad_heads, value_heads, preferred_element_type=jnp.float32
    )
    score_grad = (prob * (value_pull - row_dot[..., None])).astype(jnp.bfloat16)
    grad_queries = (
        jnp.einsum("hqk,khd->qhd", score_grad, key_heads, preferred_element_type=jnp.float32)
        * score_scale
    )
    grad_queries = grad_queries.astype(jnp.bfloat16).reshape(tok_rows, width)

    own_keys = keys.reshape(tok_rows, HEADS, head_size)
    own_values = values.reshape(tok_rows, HEADS, head_size)
    grad_keys = 0.0
    grad_values = 0.0
    for query_block, total_block, grad_block, dot_block in zip(query_blocks, total_blocks, grad_blocks, dot_blocks):
        block_queries = query_block.reshape(tok_rows, HEADS, head_size)
        block_grads = grad_block.reshape(tok_rows, HEADS, head_size)
        block_scores = (
            jnp.einsum("qhd,khd->hqk", block_queries, own_keys, preferred_element_type=jnp.float32)
            * score_scale
        )
        block_prob = jnp.exp(block_scores - total_block[..., None])
        block_pull = jnp.einsum(
            "qhd,khd->hqk", block_grads, own_values, preferred_element_type=jnp.float32
        )
        block_score_grad = (block_prob * (block_pull - dot_block[..., None])).astype(jnp.bfloat16)
        grad_keys = grad_keys + (
            jnp.einsum(
                "hqk,qhd->khd", block_score_grad, block_queries, preferred_element_type=jnp.float32
            )
            * score_scale
        )
        value_term = jnp.einsum(
            "hqk,qhd->khd",
            block_prob.astype(jnp.bfloat16),
            block_grads,
            preferred_element_type=jnp.float32,
        )
        grad_values = grad_values + value_term
    grad_keys = grad_keys.astype(jnp.bfloat16).reshape(tok_rows, width)
    grad_values = grad_values.astype(jnp.bfloat16).reshape(tok_rows, width)

    home_flat = returned.reshape(experts * capacity, width)
    branch = gate_one[:, None] * dot(pick_one, home_flat) + gate_two[:, None] * dot(
        pick_two, home_flat
    )
    mixed_out = (hidden_sum + mod_gate * branch).astype(jnp.bfloat16)
    return (
        mixed_out,
        resid_grad,
        grad_queries,
        grad_keys,
        grad_values,
        grad_w_in,
        grad_w_out,
        grad_router,
    )


def solution(mesh):
    return jax.shard_map(
        local,
        mesh=mesh,
        in_specs=(
            P(("expert", "ctx"), None),
            P(("expert", "ctx"), None),
            P(("expert", "ctx"), None),
            P(("expert", "ctx"), None),
            P("expert", None),
            P("expert", None),
            P("expert", None),
            P(),
            P("expert", None, "ctx"),
            P("expert", "ctx", None),
            P(("expert", "ctx"), None),
            P(("expert", "ctx"), None),
        ),
        out_specs=(
            P(("expert", "ctx"), None),
            P(("expert", "ctx"), None),
            P(("expert", "ctx"), None),
            P(("expert", "ctx"), None),
            P(("expert", "ctx"), None),
            P("expert", None, "ctx"),
            P("expert", "ctx", None),
            P(),
        ),
        check_vma=False,
    )
```
